32 devices in a mesh: dp: 8 (over y, x, core), ctx: 4 (over z).
Axes of the slice: x: 2, y: 2, z: 4, core: 2. Of those that a mesh axis runs over, the one named last changes fastest.
Arguments:
- query_proj: bfloat16 [8, 512, 4096], P('dp', 'ctx'), may hold values from -6 to 6
- key_proj: bfloat16 [8, 512, 4096], P('dp', 'ctx'), may hold values from -6 to 6
- value_proj: bfloat16 [8, 512, 4096], P('dp', 'ctx'), may hold values from -6 to 6
- offsets: int32 [8, 512], P('dp', 'ctx'), may hold values from 0 to 511, as said below
- filter_taps: float32 [256, 128], P(('dp', 'ctx')), may hold values from -1.2 to 1.2
- filter_decay: float32 [256], P(('dp', 'ctx')), may hold values from 0.003125 to 0.09375
- out_weight: bfloat16 [4096, 8192], P('dp', 'ctx'), may hold values from -0.09375 to 0.09375
- grad_mixed: bfloat16 [8, 512, 8192], P('dp', None, 'ctx'), may hold values from -1.5 to 1.5
Outputs:
- mixed: bfloat16 [8, 512, 8192], P('dp', None, 'ctx')
- grad_query: bfloat16 [8, 512, 4096], P('dp', 'ctx')
- grad_key: bfloat16 [8, 512, 4096], P('dp', 'ctx')
- grad_value: bfloat16 [8, 512, 4096], P('dp', 'ctx')
- grad_weight: float32 [4096, 8192], P('dp', 'ctx')
- grad_taps: float32 [256, 128], P(('dp', 'ctx'))
- grad_decay: float32 [256], P(('dp', 'ctx'))
The draws below stay inside these ranges and needn't reach their ends.
Inputs may be any that keep to these rules, and one draw needn't show every extreme that they name: offsets is 0 at the first base of every window and of every contig, and otherwise one more than at the base before.
All inputs are finite; a program needn't handle non-finite values.
Results may differ from the reference program's by a relative error of at most 0.02.
Values may be sent and summed in bfloat16 or wider, within the bound.
A program may use at most 192 MiB of HBM per device.

```python
import math
import jax
import jax.numpy as jnp
from jax import lax

D = 8192
C = 4096
GROUP = 16
TAPS = 128
ROWS = 128
G = 256
LENGTH = 512
WINDOWS = 8
N_CTX = 4


def draw_offsets(key, part):
    marks = jax.random.randint(key, (WINDOWS, LENGTH), 0, 2 * ROWS) == 0
    position = jnp.arange(LENGTH, dtype=jnp.int32)[None, :]
    window_index = jnp.arange(WINDOWS, dtype=jnp.int32)[:, None]
    marks = marks & (window_index != 0)
    starts = jnp.where(marks | (position == 0), position, jnp.zeros_like(position))
    starts = lax.cummax(starts, axis=1)
    return (position - starts).astype(jnp.int32)


def with_spikes(drawn, own_key, source, target, parts, factor):
    owner, partner = [(jnp.arange(drawn.shape[dim]) // (drawn.shape[dim] // parts)).reshape([-1 if axis == dim else 1 for axis in range(drawn.ndim)]) for dim in (source, target)]
    chosen = jax.random.permutation(own_key, parts)[partner]
    strong = (owner == chosen) | (owner == (partner + parts // 2) % parts)
    return jnp.where(strong, factor * drawn, drawn)


def shard_levels(rng, dims, shards, smallest, largest):
    def one(dim, shards_of):
        steps = jax.random.uniform(jax.random.fold_in(jax.random.fold_in(rng, 6), dim), (shards_of,), jnp.float32, smallest / len(shards), largest / len(shards))
        return jnp.repeat(jnp.exp(steps), dims[dim] // shards_of).reshape((-1,) + (1,) * (len(dims) - dim - 1))

    level = one(*shards[0])
    for cut in shards[1:]:
        level = level * one(*cut)
    return level


def noise(rng, extent, scale, reach, split=(), kind=jnp.bfloat16):
    result = jax.random.normal(rng, extent, jnp.float32) * scale
    if len(split) > 0:
        result = shard_levels(rng, extent, split, -0.22, 0.18) * result
    return jnp.clip(result, min=-reach, max=reach).astype(kind)


def gaussian_with(key, extent, width, bound, split, heavy, held_as=jnp.bfloat16):
    drawn = width * jax.random.normal(key, extent, jnp.float32)
    if split:
        drawn = drawn * shard_levels(key, extent, split, -0.22, 0.18)
    return jnp.clip(with_spikes(drawn, jax.random.fold_in(key, 3), *heavy), -bound, bound).astype(held_as)


def setup_inputs(seed: int = 0) -> dict:
    streams_of = jax.random.split(jax.random.key(seed), 9)
    return {
        "query_proj": gaussian_with(streams_of[0], (WINDOWS, LENGTH, C), 1.0, 6.0, ((0, 8), (1, 4)), (0, 2, 8, 2.0)),
        "key_proj": noise(streams_of[1], (WINDOWS, LENGTH, C), 1.0, 6.0, ((0, 8), (1, 4))),
        "value_proj": noise(streams_of[2], (WINDOWS, LENGTH, C), 1.0, 6.0, ((0, 8), (1, 4))),
        "offsets": draw_offsets(jax.random.fold_in(streams_of[8], 71), 0),
        "filter_taps": noise(streams_of[4], (G, TAPS), 0.2, 1.2, ((0, 32),), jnp.float32),
        "filter_decay": jnp.clip(jnp.exp(math.log(0.09375) - 3.4011974 * jax.random.uniform(streams_of[5], (G,), jnp.float32) ** shard_levels(streams_of[5], (G,), ((0, 32),), -0.2, 0.2)), 0.003125, 0.09375),
        "out_weight": noise(streams_of[6], (C, D), C ** -0.5, 0.09375, ((0, 8), (1, 4))),
        "grad_mixed": noise(streams_of[7], (WINDOWS, LENGTH, D), 0.25, 1.5, ((0, 8), (2, 4))),
    }


def envelope(filter_decay):
    tap_index = jnp.arange(TAPS, dtype=jnp.float32)
    return jnp.exp(-filter_decay[:, None] * tap_index[None, :])


def reference(query_proj, key_proj, value_proj, offsets, filter_taps, filter_decay, out_weight, grad_mixed):
    decay_env = envelope(filter_decay)
    filter_bf = (filter_taps * decay_env).astype(jnp.bfloat16)
    per_channel = jnp.repeat(filter_bf.astype(jnp.float32), GROUP, axis=0)
    block_cols = D // N_CTX

    def one_window(state_pair, inputs):
        weight_sum, filter_sum = state_pair
        query_win, key_win, value_win, offset_win, cotangent = inputs
        query32 = query_win.astype(jnp.float32)
        key32 = key_win.astype(jnp.float32)
        value32 = value_win.astype(jnp.float32)
        mixer_in = (key32 * value32).astype(jnp.bfloat16)
        mixer32 = mixer_in.astype(jnp.float32)

        def forward_tap(shift_by, running):
            column = lax.dynamic_index_in_dim(per_channel, shift_by, 1, keepdims=False)
            shifted = jnp.roll(mixer32, shift_by, axis=0)
            alive_rows = (offset_win >= shift_by)[:, None]
            return running + jnp.where(alive_rows, shifted * column[None, :], jnp.float32(0.0))

        conv_out = lax.fori_loop(0, TAPS, forward_tap, jnp.zeros((LENGTH, C), jnp.float32))
        gated = (query32 * conv_out).astype(jnp.bfloat16)
        mixed = jnp.dot(gated, out_weight, preferred_element_type=jnp.float32).astype(jnp.bfloat16)
        grad_gated = jnp.zeros((LENGTH, C), jnp.float32)
        for block_index in range(N_CTX):
            low_col = block_index * block_cols
            block_part = jnp.dot(cotangent[:, low_col:low_col + block_cols],
                                 out_weight[:, low_col:low_col + block_cols].T,
                                 preferred_element_type=jnp.float32)
            block_part = lax.optimization_barrier(block_part.astype(jnp.bfloat16))
            grad_gated = grad_gated + block_part.astype(jnp.float32)
        grad_query = (grad_gated * conv_out).astype(jnp.bfloat16)
        grad_conv = (grad_gated * query32).astype(jnp.bfloat16)
        grad32 = grad_conv.astype(jnp.float32)

        def backward_tap(shift_by, running):
            column = lax.dynamic_index_in_dim(per_channel, shift_by, 1, keepdims=False)
            alive_rows = (offset_win >= shift_by)[:, None]
            term_rows = jnp.where(alive_rows, grad32 * column[None, :], jnp.float32(0.0))
            return running + jnp.roll(term_rows, -shift_by, axis=0)

        grad_mixer = lax.fori_loop(0, TAPS, backward_tap, jnp.zeros((LENGTH, C), jnp.float32))
        grad_key = (grad_mixer * value32).astype(jnp.bfloat16)
        grad_value = (grad_mixer * key32).astype(jnp.bfloat16)

        def filter_tap(unused, shift_by):
            shifted = jnp.roll(mixer32, shift_by, axis=0)
            alive_rows = (offset_win >= shift_by)[:, None]
            per_chan = jnp.sum(jnp.where(alive_rows, grad32 * shifted, jnp.float32(0.0)), axis=0)
            return unused, jnp.sum(per_chan.reshape(C // GROUP, GROUP), axis=1)

        unused_out, filter_rows = lax.scan(filter_tap, jnp.float32(0.0), jnp.arange(TAPS, dtype=jnp.int32))
        weight_part = lax.dot_general(gated, cotangent, (((0,), (0,)), ((), ())),
                                      preferred_element_type=jnp.float32)
        weight_part = lax.optimization_barrier(weight_part.astype(jnp.bfloat16)).astype(jnp.float32)
        return (weight_sum + weight_part, filter_sum + filter_rows.T), (mixed, grad_query, grad_key, grad_value)

    initial = (jnp.zeros((C, D), jnp.float32), jnp.zeros((C // GROUP, TAPS), jnp.float32))
    totals, stacked = lax.scan(one_window, initial, (query_proj, key_proj, value_proj, offsets, grad_mixed))
    grad_weight, grad_filter = totals
    mixed, grad_query, grad_key, grad_value = stacked
    tap_index = jnp.arange(TAPS, dtype=jnp.float32)
    grad_taps = grad_filter * decay_env
    grad_decay = -jnp.sum(tap_index[None, :] * grad_filter * filter_taps * decay_env, axis=1)
    return (mixed, grad_query, grad_key, grad_value, grad_weight, grad_taps, grad_decay)
```

```python
import functools

import jax
import jax.numpy as jnp
from jax import lax
from jax.experimental import pallas as pl
from jax.experimental.pallas import tpu as pltpu
from jax.sharding import PartitionSpec as P

MESH = pl.DeviceIdType.MESH
F32 = jnp.float32
BF16 = jnp.bfloat16
LANES = 128


def greet(n_dp, n_ctx, me_dp, me_ctx):
    barrier = pltpu.get_barrier_semaphore()
    for step in range(1, n_ctx):
        peer = (me_dp, lax.rem(me_ctx + step, n_ctx))
        pl.semaphore_signal(barrier, inc=1, device_id=peer, device_id_type=MESH)
    for step in range(1, n_dp):
        peer = (lax.rem(me_dp + step, n_dp), me_ctx)
        pl.semaphore_signal(barrier, inc=1, device_id=peer, device_id_type=MESH)
    pl.semaphore_wait(barrier, n_ctx + n_dp - 2)


def gather_kernel(n_dp, n_ctx, x_ref, out_ref, held, send1, recv1, send2, recv2):
    me_dp, me_ctx = lax.axis_index("dp"), lax.axis_index("ctx")
    greet(n_dp, n_ctx, me_dp, me_ctx)
    held[me_dp, me_ctx] = x_ref[...]
    copies = []
    for step in range(1, n_ctx):
        copy = pltpu.make_async_remote_copy(
            src_ref=x_ref,
            dst_ref=held.at[me_dp, me_ctx],
            send_sem=send1.at[step - 1],
            recv_sem=recv1.at[step - 1],
            device_id=(me_dp, lax.rem(me_ctx + step, n_ctx)),
            device_id_type=MESH,
        )
        copy.start()
        copies.append(copy)
    for copy in copies:
        copy.wait()
    copies = []
    for step in range(1, n_dp):
        copy = pltpu.make_async_remote_copy(
            src_ref=held.at[me_dp],
            dst_ref=held.at[me_dp],
            send_sem=send2.at[step - 1],
            recv_sem=recv2.at[step - 1],
            device_id=(lax.rem(me_dp + step, n_dp), me_ctx),
            device_id_type=MESH,
        )
        copy.start()
        copies.append(copy)
    for copy in copies:
        copy.wait()
    out_ref[...] = held[...]


def gather_filters(filter_loc, n_dp, n_ctx):
    rows, taps = filter_loc.shape
    out = pl.pallas_call(
        functools.partial(gather_kernel, n_dp, n_ctx),
        out_shape=jax.ShapeDtypeStruct((n_dp, n_ctx, rows, taps), F32),
        in_specs=[pl.BlockSpec(memory_space=pltpu.VMEM)],
        out_specs=pl.BlockSpec(memory_space=pltpu.VMEM),
        scratch_shapes=[
            pltpu.VMEM((n_dp, n_ctx, rows, taps), F32),
            pltpu.SemaphoreType.DMA((n_ctx - 1,)),
            pltpu.SemaphoreType.DMA((n_ctx - 1,)),
            pltpu.SemaphoreType.DMA((n_dp - 1,)),
            pltpu.SemaphoreType.DMA((n_dp - 1,)),
        ],
        compiler_params=pltpu.CompilerParams(collective_id=0, has_side_effects=True),
    )(filter_loc)
    return out.reshape(n_dp * n_ctx * rows, taps)


def reduce_kernel(n_dp, n_ctx, x_ref, out_ref, got1, part, got2, send1, recv1, send2, recv2):
    me_dp, me_ctx = lax.axis_index("dp"), lax.axis_index("ctx")
    greet(n_dp, n_ctx, me_dp, me_ctx)
    copies = []
    for step in range(1, n_ctx):
        peer = lax.rem(me_ctx + step, n_ctx)
        copy = pltpu.make_async_remote_copy(
            src_ref=x_ref.at[peer],
            dst_ref=got1.at[step - 1],
            send_sem=send1.at[step - 1],
            recv_sem=recv1.at[step - 1],
            device_id=(me_dp, peer),
            device_id_type=MESH,
        )
        copy.start()
        copies.append(copy)
    for copy in copies:
        copy.wait()
    total = x_ref[me_ctx]
    for step in range(1, n_ctx):
        total = total + got1[step - 1]
    part[...] = total
    copies = []
    for step in range(1, n_dp):
        peer = lax.rem(me_dp + step, n_dp)
        copy = pltpu.make_async_remote_copy(
            src_ref=part.at[peer],
            dst_ref=got2.at[step - 1],
            send_sem=send2.at[step - 1],
            recv_sem=recv2.at[step - 1],
            device_id=(peer, me_ctx),
            device_id_type=MESH,
        )
        copy.start()
        copies.append(copy)
    for copy in copies:
        copy.wait()
    total = part[me_dp]
    for step in range(1, n_dp):
        total = total + got2[step - 1]
    out_ref[...] = total


def reduce_filters(grad_filter, n_dp, n_ctx):
    groups, taps = grad_filter.shape
    rows = groups // (n_dp * n_ctx)
    blocks = grad_filter.reshape(n_dp, n_ctx, rows, taps).transpose(1, 0, 2, 3)
    return pl.pallas_call(
        functools.partial(reduce_kernel, n_dp, n_ctx),
        out_shape=jax.ShapeDtypeStruct((rows, taps), F32),
        in_specs=[pl.BlockSpec(memory_space=pltpu.VMEM)],
        out_specs=pl.BlockSpec(memory_space=pltpu.VMEM),
        scratch_shapes=[
            pltpu.VMEM((n_ctx - 1, n_dp, rows, taps), F32),
            pltpu.VMEM((n_dp, rows, taps), F32),
            pltpu.VMEM((n_dp - 1, rows, taps), F32),
            pltpu.SemaphoreType.DMA((n_ctx - 1,)),
            pltpu.SemaphoreType.DMA((n_ctx - 1,)),
            pltpu.SemaphoreType.DMA((n_dp - 1,)),
            pltpu.SemaphoreType.DMA((n_dp - 1,)),
        ],
        compiler_params=pltpu.CompilerParams(collective_id=1, has_side_effects=True),
    )(blocks)


def circulant(row):
    size = row.shape[1]
    return pltpu.roll(
        jnp.broadcast_to(row, (size, size)), 0, 1, stride=1, stride_axis=0
    )


def grids(size):
    return (
        lax.broadcasted_iota(jnp.int32, (size, size), 0),
        lax.broadcasted_iota(jnp.int32, (size, size), 1),
    )


def forward_kernel(width, off_ref, filt_ref, prev_ref, mix_ref, query_ref, conv_ref, gated_ref):
    size = LANES
    t_index, u_index = grids(size)
    off = jnp.broadcast_to(off_ref[...], (size, size))
    own = (u_index <= t_index) & (t_index - u_index <= off)
    before = (u_index > t_index) & (t_index + size - u_index <= off)
    per_tile = LANES // width
    lane_group = lax.broadcasted_iota(jnp.int32, (2 * size, LANES), 1) // width
    for tile in range(mix_ref.shape[1] // LANES):
        cols = slice(tile * LANES, (tile + 1) * LANES)
        mixer = jnp.concatenate([prev_ref[:, cols], mix_ref[:, cols]], axis=0)
        total = jnp.zeros((size, LANES), F32)
        for index in range(per_tile):
            group = tile * per_tile + index
            ring = circulant(filt_ref[group : group + 1, :])
            band = jnp.concatenate(
                [jnp.where(before, ring, 0.0).astype(BF16), jnp.where(own, ring, 0.0).astype(BF16)],
                axis=1,
            )
            picked = jnp.where(lane_group == index, mixer, jnp.zeros((), BF16))
            total = total + jnp.dot(band, picked, preferred_element_type=F32)
        conv_ref[:, cols] = total
        gated_ref[:, cols] = (query_ref[:, cols].astype(F32) * total).astype(BF16)


def conv_forward(offset_col, filt_rev, previous, mixer_in, query, width, block):
    rows, chans = mixer_in.shape
    groups = block // width
    spec = pl.BlockSpec((rows, block), lambda i: (0, i))
    return pl.pallas_call(
        functools.partial(forward_kernel, width),
        grid=(chans // block,),
        out_shape=(
            jax.ShapeDtypeStruct((rows, chans), F32),
            jax.ShapeDtypeStruct((rows, chans), BF16),
        ),
        in_specs=[
            pl.BlockSpec((rows, 1), lambda i: (0, 0)),
            pl.BlockSpec((groups, rows), lambda i: (i, 0)),
            spec,
            spec,
            spec,
        ],
        out_specs=(spec, spec),
        cost_estimate=pl.CostEstimate(
            flops=4 * rows * rows * LANES * (chans // width),
            bytes_accessed=12 * rows * chans,
            transcendentals=0,
        ),
    )(offset_col, filt_rev, previous, mixer_in, query)


def backward_kernel(
    width, parts, off_row_ref, off_flip_ref, filt_ref, prev_ref, mix_ref, query_ref, conv_ref, *rest
):
    part_refs = rest[:parts]
    gquery_ref, gmix_ref, spill_ref, gfilt_ref = rest[parts:]
    size = LANES
    u_index, t_index = grids(size)
    off = jnp.broadcast_to(off_row_ref[...], (size, size))
    own = (u_index <= t_index) & (t_index - u_index <= off)
    before = (u_index > t_index) & (t_index + size - u_index <= off)
    flip_row, lag_col = grids(size)
    flip_t = size - 1 - flip_row
    off_flip = jnp.broadcast_to(off_flip_ref[...], (size, size))
    own_flip = (lag_col <= flip_t) & (flip_t - lag_col <= off_flip)
    before_flip = (lag_col > flip_t) & (flip_t + size - lag_col <= off_flip)
    flip = jnp.where(flip_row + lag_col == size - 1, 1.0, 0.0).astype(BF16)
    per_tile = LANES // width
    lane_group = lax.broadcasted_iota(jnp.int32, (size, LANES), 1) // width
    zero = jnp.zeros((), BF16)
    for tile in range(mix_ref.shape[1] // LANES):
        cols = slice(tile * LANES, (tile + 1) * LANES)
        mixer = jnp.concatenate([prev_ref[:, cols], mix_ref[:, cols]], axis=0)
        gated_grad = part_refs[0][:, cols].astype(F32)
        for ref in part_refs[1:]:
            gated_grad = gated_grad + ref[:, cols].astype(F32)
        gquery_ref[:, cols] = (gated_grad * conv_ref[:, cols]).astype(BF16)
        gconv = (gated_grad * query_ref[:, cols].astype(F32)).astype(BF16)
        flipped = jnp.dot(flip, gconv, preferred_element_type=F32).astype(BF16)
        total = jnp.zeros((2 * size, LANES), F32)
        for pair in range(per_tile // 2):
            bands, picks = [], []
            for index in (2 * pair, 2 * pair + 1):
                group = tile * per_tile + index
                ring = circulant(filt_ref[group : group + 1, :])
                bands.append(
                    jnp.concatenate(
                        [
                            jnp.where(before, ring, 0.0).astype(BF16),
                            jnp.where(own, ring, 0.0).astype(BF16),
                        ],
                        axis=0,
                    )
                )
                picks.append(jnp.where(lane_group == index, gconv, zero))
                product = lax.dot_general(
                    jnp.where(lane_group == index, flipped, zero),
                    mixer,
                    (((1,), (1,)), ((), ())),
                    preferred_element_type=F32,
                )
                folded = jnp.where(
                    own_flip,
                    product[:, size:],
                    jnp.where(before_flip, product[:, :size], 0.0),
                )
                aligned = pltpu.roll(folded, 1, 1, stride=1, stride_axis=0)
                gfilt_ref[group : group + 1, :] = jnp.sum(aligned, axis=0, keepdims=True)
            total = total + jnp.dot(
                jnp.concatenate(bands, axis=1),
                jnp.concatenate(picks, axis=0),
                preferred_element_type=F32,
            )
        spill_ref[:, cols] = total[:size].astype(BF16)
        gmix_ref[:, cols] = total[size:]


def conv_backward(
    offset_row, offset_flip, filt, previous, mixer_in, query, conv_out, parts, width, block
):
    rows, chans = mixer_in.shape
    groups = block // width
    spec = pl.BlockSpec((rows, block), lambda i: (0, i))
    filt_spec = pl.BlockSpec((groups, rows), lambda i: (i, 0))
    return pl.pallas_call(
        functools.partial(backward_kernel, width, len(parts)),
        grid=(chans // block,),
        out_shape=(
            jax.ShapeDtypeStruct((rows, chans), BF16),
            jax.ShapeDtypeStruct((rows, chans), F32),
            jax.ShapeDtypeStruct((rows, chans), BF16),
            jax.ShapeDtypeStruct((chans // width, rows), F32),
        ),
        in_specs=[
            pl.BlockSpec((1, rows), lambda i: (0, 0)),
            pl.BlockSpec((rows, 1), lambda i: (0, 0)),
            filt_spec,
            spec,
            spec,
            spec,
            spec,
        ]
        + [spec] * len(parts),
        out_specs=(spec, spec, spec, filt_spec),
        cost_estimate=pl.CostEstimate(
            flops=8 * rows * rows * LANES * (chans // width),
            bytes_accessed=28 * rows * chans,
            transcendentals=0,
        ),
    )(offset_row, offset_flip, filt, previous, mixer_in, query, conv_out, *parts)


def shifted(value, axis, by):
    length = lax.axis_size(axis)
    pairs = [(i, i + by) for i in range(length) if 0 <= i + by < length]
    return lax.ppermute(value, axis, pairs)


def rotated(value, axis, by):
    length = lax.axis_size(axis)
    return lax.ppermute(value, axis, [(i, (i + by) % length) for i in range(length)])


def mirror(rows):
    return jnp.concatenate([rows[:, :1], rows[:, :0:-1]], axis=1)


def local(
    query_proj, key_proj, value_proj, offsets, filter_taps, filter_decay, out_weight, grad_mixed
):
    n_dp, n_ctx = lax.axis_size("dp"), lax.axis_size("ctx")
    me_ctx = lax.axis_index("ctx")
    query_loc = query_proj[0]
    key_loc = key_proj[0]
    value_loc = value_proj[0]
    offset_loc = offsets[0]
    cotangent = grad_mixed[0]
    rows, chans = query_loc.shape
    taps = filter_taps.shape[1]

    weight_full = lax.all_gather(out_weight, "dp", axis=0, tiled=True)
    mixer_in = (key_loc.astype(F32) * value_loc.astype(F32)).astype(BF16)
    previous = shifted(mixer_in, "ctx", 1)

    tap_index = jnp.arange(taps, dtype=F32)
    decay_env = jnp.exp(-filter_decay[:, None] * tap_index[None, :])
    filter_loc = (filter_taps * decay_env).astype(BF16).astype(F32)
    filt = gather_filters(filter_loc, n_dp, n_ctx)
    width = chans // filt.shape[0]
    block = 2 * LANES

    conv_out, gated = conv_forward(
        offset_loc[:, None], mirror(filt), previous, mixer_in, query_loc, width, block
    )
    gated_full = lax.dynamic_update_slice(
        jnp.zeros((n_ctx * rows, chans), BF16), gated, (me_ctx * rows, 0)
    )
    for step in range(1, n_ctx):
        came = rotated(gated, "ctx", step)
        source = lax.rem(me_ctx - step + n_ctx, n_ctx)
        gated_full = lax.dynamic_update_slice(gated_full, came, (source * rows, 0))

    grad_part = lax.dot_general(
        cotangent, weight_full, (((1,), (1,)), ((), ())), preferred_element_type=F32
    ).astype(BF16)
    parts = [lax.dynamic_slice(grad_part, (me_ctx * rows, 0), (rows, chans))]
    for step in range(1, n_ctx):
        target = lax.rem(me_ctx + step, n_ctx)
        sent = lax.dynamic_slice(grad_part, (target * rows, 0), (rows, chans))
        parts.append(rotated(sent, "ctx", step))

    grad_weight = lax.psum_scatter(
        lax.dot_general(
            gated_full, cotangent, (((0,), (0,)), ((), ())), preferred_element_type=F32
        ).astype(BF16),
        "dp",
        scatter_dimension=0,
        tiled=True,
    ).astype(F32)
    mixed = jnp.dot(gated_full, weight_full, preferred_element_type=F32).astype(BF16)

    grad_query, grad_own, spill, lag_sums = conv_backward(
        offset_loc[None, :],
        offset_loc[::-1][:, None],
        filt,
        previous,
        mixer_in,
        query_loc,
        conv_out,
        parts,
        width,
        block,
    )
    grad_mixer = grad_own + shifted(spill, "ctx", -1).astype(F32)
    grad_key = (grad_mixer * value_loc.astype(F32)).astype(BF16)
    grad_value = (grad_mixer * key_loc.astype(F32)).astype(BF16)

    grad_filter = mirror(reduce_filters(lag_sums, n_dp, n_ctx))
    grad_taps = grad_filter * decay_env
    grad_decay = -jnp.sum(tap_index[None, :] * grad_filter * filter_taps * decay_env, axis=1)
    return (
        mixed[None],
        grad_query[None],
        grad_key[None],
        grad_value[None],
        grad_weight,
        grad_taps,
        grad_decay,
    )


def solution(mesh):
    in_specs = (
        P("dp", "ctx", None),
        P("dp", "ctx", None),
        P("dp", "ctx", None),
        P("dp", "ctx"),
        P(("dp", "ctx"), None),
        P(("dp", "ctx")),
        P("dp", "ctx"),
        P("dp", None, "ctx"),
    )
    out_specs = (
        P("dp", None, "ctx"),
        P("dp", "ctx", None),
        P("dp", "ctx", None),
        P("dp", "ctx", None),
        P("dp", "ctx"),
        P(("dp", "ctx"), None),
        P(("dp", "ctx")),
    )
    return jax.shard_map(local, mesh=mesh, in_specs=in_specs, out_specs=out_specs, check_vma=False)
```

```python
import functools

import jax
import jax.numpy as jnp
from jax import lax
from jax.experimental import pallas as pl
from jax.experimental.pallas import tpu as pltpu
from jax.sharding import PartitionSpec as P

MESH = pl.DeviceIdType.MESH
F32 = jnp.float32
BF16 = jnp.bfloat16
LANES = 128


def greet(n_dp, n_ctx, me_dp, me_ctx):
    barrier = pltpu.get_barrier_semaphore()
    for step in range(1, n_ctx):
        peer = (me_dp, lax.rem(me_ctx + step, n_ctx))
        pl.semaphore_signal(barrier, inc=1, device_id=peer, device_id_type=MESH)
    for step in range(1, n_dp):
        peer = (lax.rem(me_dp + step, n_dp), me_ctx)
        pl.semaphore_signal(barrier, inc=1, device_id=peer, device_id_type=MESH)
    pl.semaphore_wait(barrier, n_ctx + n_dp - 2)


def gather_kernel(n_dp, n_ctx, x_ref, out_ref, held, send1, recv1, send2, recv2):
    me_dp, me_ctx = lax.axis_index("dp"), lax.axis_index("ctx")
    greet(n_dp, n_ctx, me_dp, me_ctx)
    held[me_dp, me_ctx] = x_ref[...]
    copies = []
    for step in range(1, n_ctx):
        copy = pltpu.make_async_remote_copy(
            src_ref=x_ref,
            dst_ref=held.at[me_dp, me_ctx],
            send_sem=send1.at[step - 1],
            recv_sem=recv1.at[step - 1],
            device_id=(me_dp, lax.rem(me_ctx + step, n_ctx)),
            device_id_type=MESH,
        )
        copy.start()
        copies.append(copy)
    for copy in copies:
        copy.wait()
    copies = []
    for step in range(1, n_dp):
        copy = pltpu.make_async_remote_copy(
            src_ref=held.at[me_dp],
            dst_ref=held.at[me_dp],
            send_sem=send2.at[step - 1],
            recv_sem=recv2.at[step - 1],
            device_id=(lax.rem(me_dp + step, n_dp), me_ctx),
            device_id_type=MESH,
        )
        copy.start()
        copies.append(copy)
    for copy in copies:
        copy.wait()
    out_ref[...] = held[...]


def gather_filters(filter_loc, n_dp, n_ctx):
    rows, taps = filter_loc.shape
    out = pl.pallas_call(
        functools.partial(gather_kernel, n_dp, n_ctx),
        out_shape=jax.ShapeDtypeStruct((n_dp, n_ctx, rows, taps), F32),
        in_specs=[pl.BlockSpec(memory_space=pltpu.VMEM)],
        out_specs=pl.BlockSpec(memory_space=pltpu.VMEM),
        scratch_shapes=[
            pltpu.VMEM((n_dp, n_ctx, rows, taps), F32),
            pltpu.SemaphoreType.DMA((n_ctx - 1,)),
            pltpu.SemaphoreType.DMA((n_ctx - 1,)),
            pltpu.SemaphoreType.DMA((n_dp - 1,)),
            pltpu.SemaphoreType.DMA((n_dp - 1,)),
        ],
        compiler_params=pltpu.CompilerParams(collective_id=0, has_side_effects=True),
    )(filter_loc)
    return out.reshape(n_dp * n_ctx * rows, taps)


def reduce_kernel(n_dp, n_ctx, x_ref, out_ref, got1, part, got2, send1, recv1, send2, recv2):
    me_dp, me_ctx = lax.axis_index("dp"), lax.axis_index("ctx")
    greet(n_dp, n_ctx, me_dp, me_ctx)
    copies = []
    for step in range(1, n_ctx):
        peer = lax.rem(me_ctx + step, n_ctx)
        copy = pltpu.make_async_remote_copy(
            src_ref=x_ref.at[peer],
            dst_ref=got1.at[step - 1],
            send_sem=send1.at[step - 1],
            recv_sem=recv1.at[step - 1],
            device_id=(me_dp, peer),
            device_id_type=MESH,
        )
        copy.start()
        copies.append(copy)
    for copy in copies:
        copy.wait()
    total = x_ref[me_ctx]
    for step in range(1, n_ctx):
        total = total + got1[step - 1]
    part[...] = total
    copies = []
    for step in range(1, n_dp):
        peer = lax.rem(me_dp + step, n_dp)
        copy = pltpu.make_async_remote_copy(
            src_ref=part.at[peer],
            dst_ref=got2.at[step - 1],
            send_sem=send2.at[step - 1],
            recv_sem=recv2.at[step - 1],
            device_id=(peer, me_ctx),
            device_id_type=MESH,
        )
        copy.start()
        copies.append(copy)
    for copy in copies:
        copy.wait()
    total = part[me_dp]
    for step in range(1, n_dp):
        total = total + got2[step - 1]
    out_ref[...] = total


def reduce_filters(grad_filter, n_dp, n_ctx):
    groups, taps = grad_filter.shape
    rows = groups // (n_dp * n_ctx)
    blocks = grad_filter.reshape(n_dp, n_ctx, rows, taps).transpose(1, 0, 2, 3)
    return pl.pallas_call(
        functools.partial(reduce_kernel, n_dp, n_ctx),
        out_shape=jax.ShapeDtypeStruct((rows, taps), F32),
        in_specs=[pl.BlockSpec(memory_space=pltpu.VMEM)],
        out_specs=pl.BlockSpec(memory_space=pltpu.VMEM),
        scratch_shapes=[
            pltpu.VMEM((n_ctx - 1, n_dp, rows, taps), F32),
            pltpu.VMEM((n_dp, rows, taps), F32),
            pltpu.VMEM((n_dp - 1, rows, taps), F32),
            pltpu.SemaphoreType.DMA((n_ctx - 1,)),
            pltpu.SemaphoreType.DMA((n_ctx - 1,)),
            pltpu.SemaphoreType.DMA((n_dp - 1,)),
            pltpu.SemaphoreType.DMA((n_dp - 1,)),
        ],
        compiler_params=pltpu.CompilerParams(collective_id=1, has_side_effects=True),
    )(blocks)


def circulant(row):
    size = row.shape[1]
    return pltpu.roll(
        jnp.broadcast_to(row, (size, size)), 0, 1, stride=1, stride_axis=0
    )


def grids(size):
    return (
        lax.broadcasted_iota(jnp.int32, (size, size), 0),
        lax.broadcasted_iota(jnp.int32, (size, size), 1),
    )


def forward_kernel(width, off_ref, filt_ref, prev_ref, mix_ref, query_ref, conv_ref, gated_ref):
    size = LANES
    t_index, u_index = grids(size)
    off = jnp.broadcast_to(off_ref[...], (size, size))
    own = (u_index <= t_index) & (t_index - u_index <= off)
    before = (u_index > t_index) & (t_index + size - u_index <= off)
    per_tile = LANES // width
    lane_group = lax.broadcasted_iota(jnp.int32, (2 * size, LANES), 1) // width
    for tile in range(mix_ref.shape[1] // LANES):
        cols = slice(tile * LANES, (tile + 1) * LANES)
        mixer = jnp.concatenate([prev_ref[:, cols], mix_ref[:, cols]], axis=0)
        total = jnp.zeros((size, LANES), F32)
        for index in range(per_tile):
            group = tile * per_tile + index
            ring = circulant(filt_ref[group : group + 1, :])
            band = jnp.concatenate(
                [jnp.where(before, ring, 0.0).astype(BF16), jnp.where(own, ring, 0.0).astype(BF16)],
                axis=1,
            )
            picked = jnp.where(lane_group == index, mixer, jnp.zeros((), BF16))
            total = total + jnp.dot(band, picked, preferred_element_type=F32)
        conv_ref[:, cols] = total
        gated_ref[:, cols] = (query_ref[:, cols].astype(F32) * total).astype(BF16)


def conv_forward(offset_col, filt_rev, previous, mixer_in, query, width, block):
    rows, chans = mixer_in.shape
    groups = block // width
    spec = pl.BlockSpec((rows, block), lambda i: (0, i))
    return pl.pallas_call(
        functools.partial(forward_kernel, width),
        grid=(chans // block,),
        out_shape=(
            jax.ShapeDtypeStruct((rows, chans), F32),
            jax.ShapeDtypeStruct((rows, chans), BF16),
        ),
        in_specs=[
            pl.BlockSpec((rows, 1), lambda i: (0, 0)),
            pl.BlockSpec((groups, rows), lambda i: (i, 0)),
            spec,
            spec,
            spec,
        ],
        out_specs=(spec, spec),
        cost_estimate=pl.CostEstimate(
            flops=4 * rows * rows * LANES * (chans // width),
            bytes_accessed=12 * rows * chans,
            transcendentals=0,
        ),
    )(offset_col, filt_rev, previous, mixer_in, query)


def backward_kernel(
    width, parts, off_row_ref, off_flip_ref, filt_ref, prev_ref, mix_ref, query_ref, conv_ref, *rest
):
    part_refs = rest[:parts]
    gquery_ref, gmix_ref, spill_ref, gfilt_ref = rest[parts:]
    size = LANES
    u_index, t_index = grids(size)
    off = jnp.broadcast_to(off_row_ref[...], (size, size))
    own = (u_index <= t_index) & (t_index - u_index <= off)
    before = (u_index > t_index) & (t_index + size - u_index <= off)
    flip_row, lag_col = grids(size)
    flip_t = size - 1 - flip_row
    off_flip = jnp.broadcast_to(off_flip_ref[...], (size, size))
    own_flip = (lag_col <= flip_t) & (flip_t - lag_col <= off_flip)
    before_flip = (lag_col > flip_t) & (flip_t + size - lag_col <= off_flip)
    flip = jnp.where(flip_row + lag_col == size - 1, 1.0, 0.0).astype(BF16)
    per_tile = LANES // width
    lane_group = lax.broadcasted_iota(jnp.int32, (size, LANES), 1) // width
    zero = jnp.zeros((), BF16)
    for tile in range(mix_ref.shape[1] // LANES):
        cols = slice(tile * LANES, (tile + 1) * LANES)
        mixer = jnp.concatenate([prev_ref[:, cols], mix_ref[:, cols]], axis=0)
        gated_grad = part_refs[0][:, cols].astype(F32)
        for ref in part_refs[1:]:
            gated_grad = gated_grad + ref[:, cols].astype(F32)
        gquery_ref[:, cols] = (gated_grad * conv_ref[:, cols]).astype(BF16)
        gconv = (gated_grad * query_ref[:, cols].astype(F32)).astype(BF16)
        flipped = jnp.dot(flip, gconv, preferred_element_type=F32).astype(BF16)
        total = jnp.zeros((2 * size, LANES), F32)
        for pair in range(per_tile // 2):
            bands, picks = [], []
            for index in (2 * pair, 2 * pair + 1):
                group = tile * per_tile + index
                ring = circulant(filt_ref[group : group + 1, :])
                bands.append(
                    jnp.concatenate(
                        [
                            jnp.where(before, ring, 0.0).astype(BF16),
                            jnp.where(own, ring, 0.0).astype(BF16),
                        ],
                        axis=0,
                    )
                )
                picks.append(jnp.where(lane_group == index, gconv, zero))
                product = lax.dot_general(
                    jnp.where(lane_group == index, flipped, zero),
                    mixer,
                    (((1,), (1,)), ((), ())),
                    preferred_element_type=F32,
                )
                folded = jnp.where(
                    own_flip,
                    product[:, size:],
                    jnp.where(before_flip, product[:, :size], 0.0),
                )
                aligned = pltpu.roll(folded, 1, 1, stride=1, stride_axis=0)
                gfilt_ref[group : group + 1, :] = jnp.sum(aligned, axis=0, keepdims=True)
            total = total + jnp.dot(
                jnp.concatenate(bands, axis=1),
                jnp.concatenate(picks, axis=0),
                preferred_element_type=F32,
            )
        spill_ref[:, cols] = total[:size].astype(BF16)
        gmix_ref[:, cols] = total[size:]


def conv_backward(
    offset_row, offset_flip, filt, previous, mixer_in, query, conv_out, parts, width, block
):
    rows, chans = mixer_in.shape
    groups = block // width
    spec = pl.BlockSpec((rows, block), lambda i: (0, i))
    filt_spec = pl.BlockSpec((groups, rows), lambda i: (i, 0))
    return pl.pallas_call(
        functools.partial(backward_kernel, width, len(parts)),
        grid=(chans // block,),
        out_shape=(
            jax.ShapeDtypeStruct((rows, chans), BF16),
            jax.ShapeDtypeStruct((rows, chans), F32),
            jax.ShapeDtypeStruct((rows, chans), BF16),
            jax.ShapeDtypeStruct((chans // width, rows), F32),
        ),
        in_specs=[
            pl.BlockSpec((1, rows), lambda i: (0, 0)),
            pl.BlockSpec((rows, 1), lambda i: (0, 0)),
            filt_spec,
            spec,
            spec,
            spec,
            spec,
        ]
        + [spec] * len(parts),
        out_specs=(spec, spec, spec, filt_spec),
        cost_estimate=pl.CostEstimate(
            flops=8 * rows * rows * LANES * (chans // width),
            bytes_accessed=28 * rows * chans,
            transcendentals=0,
        ),
    )(offset_row, offset_flip, filt, previous, mixer_in, query, conv_out, *parts)


def shifted(value, axis, by):
    length = lax.axis_size(axis)
    pairs = [(i, i + by) for i in range(length) if 0 <= i + by < length]
    return lax.ppermute(value, axis, pairs)


def rotated(value, axis, by):
    length = lax.axis_size(axis)
    return lax.ppermute(value, axis, [(i, (i + by) % length) for i in range(length)])


def mirror(rows):
    return jnp.concatenate([rows[:, :1], rows[:, :0:-1]], axis=1)


def local(
    query_proj, key_proj, value_proj, offsets, filter_taps, filter_decay, out_weight, grad_mixed
):
    n_dp, n_ctx = lax.axis_size("dp"), lax.axis_size("ctx")
    me_ctx = lax.axis_index("ctx")
    query_loc = query_proj[0]
    key_loc = key_proj[0]
    value_loc = value_proj[0]
    offset_loc = offsets[0]
    cotangent = grad_mixed[0]
    rows, chans = query_loc.shape
    taps = filter_taps.shape[1]

    weight_full = lax.all_gather(out_weight, "dp", axis=0, tiled=True)
    mixer_in = (key_loc.astype(F32) * value_loc.astype(F32)).astype(BF16)
    previous = shifted(mixer_in, "ctx", 1)

    tap_index = jnp.arange(taps, dtype=F32)
    decay_env = jnp.exp(-filter_decay[:, None] * tap_index[None, :])
    filter_loc = (filter_taps * decay_env).astype(BF16).astype(F32)
    filt = gather_filters(filter_loc, n_dp, n_ctx)
    width = chans // filt.shape[0]
    block = 2 * LANES

    conv_out, gated = conv_forward(
        offset_loc[:, None], mirror(filt), previous, mixer_in, query_loc, width, block
    )
    came = [rotated(gated, "ctx", step) for step in range(1, n_ctx)]

    grad_part = lax.dot_general(
        cotangent, weight_full, (((1,), (1,)), ((), ())), preferred_element_type=F32
    ).astype(BF16)
    parts = [lax.dynamic_slice(grad_part, (me_ctx * rows, 0), (rows, chans))]
    for step in range(1, n_ctx):
        target = lax.rem(me_ctx + step, n_ctx)
        sent = lax.dynamic_slice(grad_part, (target * rows, 0), (rows, chans))
        parts.append(rotated(sent, "ctx", step))

    gated, _ = lax.optimization_barrier((gated, grad_part))
    gated_full = lax.dynamic_update_slice(
        jnp.zeros((n_ctx * rows, chans), BF16), gated, (me_ctx * rows, 0)
    )
    for step in range(1, n_ctx):
        source = lax.rem(me_ctx - step + n_ctx, n_ctx)
        gated_full = lax.dynamic_update_slice(gated_full, came[step - 1], (source * rows, 0))

    weight_part = lax.dot_general(
        gated_full, cotangent, (((0,), (0,)), ((), ())), preferred_element_type=F32
    ).astype(BF16)
    gated_full, weight_part = lax.optimization_barrier((gated_full, weight_part))
    weight_sum = lax.psum_scatter(weight_part, "dp", scatter_dimension=0, tiled=True)
    mixed = jnp.dot(gated_full, weight_full, preferred_element_type=F32).astype(BF16)
    mixed, parts = lax.optimization_barrier((mixed, parts))

    grad_query, grad_own, spill, lag_sums = conv_backward(
        offset_loc[None, :],
        offset_loc[::-1][:, None],
        filt,
        previous,
        mixer_in,
        query_loc,
        conv_out,
        parts,
        width,
        block,
    )
    grad_mixer = grad_own + shifted(spill, "ctx", -1).astype(F32)
    grad_key = (grad_mixer * value_loc.astype(F32)).astype(BF16)
    grad_value = (grad_mixer * key_loc.astype(F32)).astype(BF16)

    grad_filter = mirror(reduce_filters(lag_sums, n_dp, n_ctx))
    grad_taps = grad_filter * decay_env
    grad_decay = -jnp.sum(tap_index[None, :] * grad_filter * filter_taps * decay_env, axis=1)
    weight_sum, grad_key, grad_value, grad_decay = lax.optimization_barrier(
        (weight_sum, grad_key, grad_value, grad_decay)
    )
    grad_weight = weight_sum.astype(F32)
    return (
        mixed[None],
        grad_query[None],
        grad_key[None],
        grad_value[None],
        grad_weight,
        grad_taps,
        grad_decay,
    )


def solution(mesh):
    in_specs = (
        P("dp", "ctx", None),
        P("dp", "ctx", None),
        P("dp", "ctx", None),
        P("dp", "ctx"),
        P(("dp", "ctx"), None),
        P(("dp", "ctx")),
        P("dp", "ctx"),
        P("dp", None, "ctx"),
    )
    out_specs = (
        P("dp", None, "ctx"),
        P("dp", "ctx", None),
        P("dp", "ctx", None),
        P("dp", "ctx", None),
        P("dp", "ctx"),
        P(("dp", "ctx"), None),
        P(("dp", "ctx")),
    )
    return jax.shard_map(local, mesh=mesh, in_specs=in_specs, out_specs=out_specs, check_vma=False)
```

```python
import functools

import jax
import jax.numpy as jnp
from jax import lax
from jax.experimental import pallas as pl
from jax.experimental.pallas import tpu as pltpu
from jax.sharding import PartitionSpec as P

MESH = pl.DeviceIdType.MESH
F32 = jnp.float32
BF16 = jnp.bfloat16
LANES = 128


def greet(n_dp, n_ctx, me_dp, me_ctx):
    barrier = pltpu.get_barrier_semaphore()
    for step in range(1, n_ctx):
        peer = (me_dp, lax.rem(me_ctx + step, n_ctx))
        pl.semaphore_signal(barrier, inc=1, device_id=peer, device_id_type=MESH)
    for step in range(1, n_dp):
        peer = (lax.rem(me_dp + step, n_dp), me_ctx)
        pl.semaphore_signal(barrier, inc=1, device_id=peer, device_id_type=MESH)
    pl.semaphore_wait(barrier, n_ctx + n_dp - 2)


def gather_kernel(n_dp, n_ctx, x_ref, out_ref, held, send1, recv1, send2, recv2):
    me_dp, me_ctx = lax.axis_index("dp"), lax.axis_index("ctx")
    greet(n_dp, n_ctx, me_dp, me_ctx)
    held[me_dp, me_ctx] = x_ref[...]
    copies = []
    for step in range(1, n_ctx):
        copy = pltpu.make_async_remote_copy(
            src_ref=x_ref,
            dst_ref=held.at[me_dp, me_ctx],
            send_sem=send1.at[step - 1],
            recv_sem=recv1.at[step - 1],
            device_id=(me_dp, lax.rem(me_ctx + step, n_ctx)),
            device_id_type=MESH,
        )
        copy.start()
        copies.append(copy)
    for copy in copies:
        copy.wait()
    copies = []
    for step in range(1, n_dp):
        copy = pltpu.make_async_remote_copy(
            src_ref=held.at[me_dp],
            dst_ref=held.at[me_dp],
            send_sem=send2.at[step - 1],
            recv_sem=recv2.at[step - 1],
            device_id=(lax.rem(me_dp + step, n_dp), me_ctx),
            device_id_type=MESH,
        )
        copy.start()
        copies.append(copy)
    for copy in copies:
        copy.wait()
    out_ref[...] = held[...]


def gather_filters(filter_loc, n_dp, n_ctx):
    rows, taps = filter_loc.shape
    out = pl.pallas_call(
        functools.partial(gather_kernel, n_dp, n_ctx),
        out_shape=jax.ShapeDtypeStruct((n_dp, n_ctx, rows, taps), F32),
        in_specs=[pl.BlockSpec(memory_space=pltpu.VMEM)],
        out_specs=pl.BlockSpec(memory_space=pltpu.VMEM),
        scratch_shapes=[
            pltpu.VMEM((n_dp, n_ctx, rows, taps), F32),
            pltpu.SemaphoreType.DMA((n_ctx - 1,)),
            pltpu.SemaphoreType.DMA((n_ctx - 1,)),
            pltpu.SemaphoreType.DMA((n_dp - 1,)),
            pltpu.SemaphoreType.DMA((n_dp - 1,)),
        ],
        compiler_params=pltpu.CompilerParams(collective_id=0, has_side_effects=True),
    )(filter_loc)
    return out.reshape(n_dp * n_ctx * rows, taps)


def reduce_kernel(n_dp, n_ctx, x_ref, out_ref, got1, part, got2, send1, recv1, send2, recv2):
    me_dp, me_ctx = lax.axis_index("dp"), lax.axis_index("ctx")
    greet(n_dp, n_ctx, me_dp, me_ctx)
    copies = []
    for step in range(1, n_ctx):
        peer = lax.rem(me_ctx + step, n_ctx)
        copy = pltpu.make_async_remote_copy(
            src_ref=x_ref.at[peer],
            dst_ref=got1.at[step - 1],
            send_sem=send1.at[step - 1],
            recv_sem=recv1.at[step - 1],
            device_id=(me_dp, peer),
            device_id_type=MESH,
        )
        copy.start()
        copies.append(copy)
    for copy in copies:
        copy.wait()
    total = x_ref[me_ctx]
    for step in range(1, n_ctx):
        total = total + got1[step - 1]
    part[...] = total
    copies = []
    for step in range(1, n_dp):
        peer = lax.rem(me_dp + step, n_dp)
        copy = pltpu.make_async_remote_copy(
            src_ref=part.at[peer],
            dst_ref=got2.at[step - 1],
            send_sem=send2.at[step - 1],
            recv_sem=recv2.at[step - 1],
            device_id=(peer, me_ctx),
            device_id_type=MESH,
        )
        copy.start()
        copies.append(copy)
    for copy in copies:
        copy.wait()
    total = part[me_dp]
    for step in range(1, n_dp):
        total = total + got2[step - 1]
    out_ref[...] = total


def reduce_filters(grad_filter, n_dp, n_ctx):
    groups, taps = grad_filter.shape
    rows = groups // (n_dp * n_ctx)
    blocks = grad_filter.reshape(n_dp, n_ctx, rows, taps).transpose(1, 0, 2, 3)
    return pl.pallas_call(
        functools.partial(reduce_kernel, n_dp, n_ctx),
        out_shape=jax.ShapeDtypeStruct((rows, taps), F32),
        in_specs=[pl.BlockSpec(memory_space=pltpu.VMEM)],
        out_specs=pl.BlockSpec(memory_space=pltpu.VMEM),
        scratch_shapes=[
            pltpu.VMEM((n_ctx - 1, n_dp, rows, taps), F32),
            pltpu.VMEM((n_dp, rows, taps), F32),
            pltpu.VMEM((n_dp - 1, rows, taps), F32),
            pltpu.SemaphoreType.DMA((n_ctx - 1,)),
            pltpu.SemaphoreType.DMA((n_ctx - 1,)),
            pltpu.SemaphoreType.DMA((n_dp - 1,)),
            pltpu.SemaphoreType.DMA((n_dp - 1,)),
        ],
        compiler_params=pltpu.CompilerParams(collective_id=1, has_side_effects=True),
    )(blocks)


def circulant(row):
    size = row.shape[1]
    return pltpu.roll(
        jnp.broadcast_to(row, (size, size)), 0, 1, stride=1, stride_axis=0
    )


def grids(size):
    return (
        lax.broadcasted_iota(jnp.int32, (size, size), 0),
        lax.broadcasted_iota(jnp.int32, (size, size), 1),
    )


def forward_kernel(width, off_ref, filt_ref, prev_ref, mix_ref, query_ref, conv_ref, gated_ref):
    size = LANES
    t_index, u_index = grids(size)
    off = jnp.broadcast_to(off_ref[...], (size, size))
    own = (u_index <= t_index) & (t_index - u_index <= off)
    before = (u_index > t_index) & (t_index + size - u_index <= off)
    per_tile = LANES // width
    lane_group = lax.broadcasted_iota(jnp.int32, (2 * size, LANES), 1) // width
    for tile in range(mix_ref.shape[1] // LANES):
        cols = slice(tile * LANES, (tile + 1) * LANES)
        mixer = jnp.concatenate([prev_ref[:, cols], mix_ref[:, cols]], axis=0)
        total = jnp.zeros((size, LANES), F32)
        for index in range(per_tile):
            group = tile * per_tile + index
            ring = circulant(filt_ref[group : group + 1, :])
            band = jnp.concatenate(
                [jnp.where(before, ring, 0.0).astype(BF16), jnp.where(own, ring, 0.0).astype(BF16)],
                axis=1,
            )
            picked = jnp.where(lane_group == index, mixer, jnp.zeros((), BF16))
            total = total + jnp.dot(band, picked, preferred_element_type=F32)
        conv_ref[:, cols] = total
        gated_ref[:, cols] = (query_ref[:, cols].astype(F32) * total).astype(BF16)


def conv_forward(offset_col, filt_rev, previous, mixer_in, query, width, block):
    rows, chans = mixer_in.shape
    groups = block // width
    spec = pl.BlockSpec((rows, block), lambda i: (0, i))
    return pl.pallas_call(
        functools.partial(forward_kernel, width),
        grid=(chans // block,),
        out_shape=(
            jax.ShapeDtypeStruct((rows, chans), F32),
            jax.ShapeDtypeStruct((rows, chans), BF16),
        ),
        in_specs=[
            pl.BlockSpec((rows, 1), lambda i: (0, 0)),
            pl.BlockSpec((groups, rows), lambda i: (i, 0)),
            spec,
            spec,
            spec,
        ],
        out_specs=(spec, spec),
        cost_estimate=pl.CostEstimate(
            flops=4 * rows * rows * LANES * (chans // width),
            bytes_accessed=12 * rows * chans,
            transcendentals=0,
        ),
    )(offset_col, filt_rev, previous, mixer_in, query)


def backward_kernel(
    width, parts, off_row_ref, off_flip_ref, filt_ref, prev_ref, mix_ref, query_ref, conv_ref, *rest
):
    part_refs = rest[:parts]
    gquery_ref, gmix_ref, spill_ref, gfilt_ref = rest[parts:]
    size = LANES
    u_index, t_index = grids(size)
    off = jnp.broadcast_to(off_row_ref[...], (size, size))
    own = (u_index <= t_index) & (t_index - u_index <= off)
    before = (u_index > t_index) & (t_index + size - u_index <= off)
    flip_row, lag_col = grids(size)
    flip_t = size - 1 - flip_row
    off_flip = jnp.broadcast_to(off_flip_ref[...], (size, size))
    own_flip = (lag_col <= flip_t) & (flip_t - lag_col <= off_flip)
    before_flip = (lag_col > flip_t) & (flip_t + size - lag_col <= off_flip)
    flip = jnp.where(flip_row + lag_col == size - 1, 1.0, 0.0).astype(BF16)
    per_tile = LANES // width
    lane_group = lax.broadcasted_iota(jnp.int32, (size, LANES), 1) // width
    zero = jnp.zeros((), BF16)
    for tile in range(mix_ref.shape[1] // LANES):
        cols = slice(tile * LANES, (tile + 1) * LANES)
        mixer = jnp.concatenate([prev_ref[:, cols], mix_ref[:, cols]], axis=0)
        gated_grad = part_refs[0][:, cols].astype(F32)
        for ref in part_refs[1:]:
            gated_grad = gated_grad + ref[:, cols].astype(F32)
        gquery_ref[:, cols] = (gated_grad * conv_ref[:, cols]).astype(BF16)
        gconv = (gated_grad * query_ref[:, cols].astype(F32)).astype(BF16)
        flipped = jnp.dot(flip, gconv, preferred_element_type=F32).astype(BF16)
        total = jnp.zeros((2 * size, LANES), F32)
        for pair in range(per_tile // 2):
            bands, picks = [], []
            for index in (2 * pair, 2 * pair + 1):
                group = tile * per_tile + index
                ring = circulant(filt_ref[group : group + 1, :])
                bands.append(
                    jnp.concatenate(
                        [
                            jnp.where(before, ring, 0.0).astype(BF16),
                            jnp.where(own, ring, 0.0).astype(BF16),
                        ],
                        axis=0,
                    )
                )
                picks.append(jnp.where(lane_group == index, gconv, zero))
                product = lax.dot_general(
                    jnp.where(lane_group == index, flipped, zero),
                    mixer,
                    (((1,), (1,)), ((), ())),
                    preferred_element_type=F32,
                )
                folded = jnp.where(
                    own_flip,
                    product[:, size:],
                    jnp.where(before_flip, product[:, :size], 0.0),
                )
                aligned = pltpu.roll(folded, 1, 1, stride=1, stride_axis=0)
                gfilt_ref[group : group + 1, :] = jnp.sum(aligned, axis=0, keepdims=True)
            total = total + jnp.dot(
                jnp.concatenate(bands, axis=1),
                jnp.concatenate(picks, axis=0),
                preferred_element_type=F32,
            )
        spill_ref[:, cols] = total[:size].astype(BF16)
        gmix_ref[:, cols] = total[size:]


def conv_backward(
    offset_row, offset_flip, filt, previous, mixer_in, query, conv_out, parts, width, block
):
    rows, chans = mixer_in.shape
    groups = block // width
    spec = pl.BlockSpec((rows, block), lambda i: (0, i))
    filt_spec = pl.BlockSpec((groups, rows), lambda i: (i, 0))
    return pl.pallas_call(
        functools.partial(backward_kernel, width, len(parts)),
        grid=(chans // block,),
        out_shape=(
            jax.ShapeDtypeStruct((rows, chans), BF16),
            jax.ShapeDtypeStruct((rows, chans), F32),
            jax.ShapeDtypeStruct((rows, chans), BF16),
            jax.ShapeDtypeStruct((chans // width, rows), F32),
        ),
        in_specs=[
            pl.BlockSpec((1, rows), lambda i: (0, 0)),
            pl.BlockSpec((rows, 1), lambda i: (0, 0)),
            filt_spec,
            spec,
            spec,
            spec,
            spec,
        ]
        + [spec] * len(parts),
        out_specs=(spec, spec, spec, filt_spec),
        cost_estimate=pl.CostEstimate(
            flops=8 * rows * rows * LANES * (chans // width),
            bytes_accessed=28 * rows * chans,
            transcendentals=0,
        ),
    )(offset_row, offset_flip, filt, previous, mixer_in, query, conv_out, *parts)


def shifted(value, axis, by):
    length = lax.axis_size(axis)
    pairs = [(i, i + by) for i in range(length) if 0 <= i + by < length]
    return lax.ppermute(value, axis, pairs)


def hop(value, by, sends):
    length = lax.axis_size("ctx")
    pairs = [(i, i + by) for i in range(length) if 0 <= i + by < length and sends(i)]
    return lax.ppermute(value, "ctx", pairs)


def mirror(rows):
    return jnp.concatenate([rows[:, :1], rows[:, :0:-1]], axis=1)


def local(
    query_proj, key_proj, value_proj, offsets, filter_taps, filter_decay, out_weight, grad_mixed
):
    n_dp, n_ctx = lax.axis_size("dp"), lax.axis_size("ctx")
    me_ctx = lax.axis_index("ctx")
    query_loc = query_proj[0]
    key_loc = key_proj[0]
    value_loc = value_proj[0]
    offset_loc = offsets[0]
    cotangent = grad_mixed[0]
    rows, chans = query_loc.shape
    taps = filter_taps.shape[1]

    weight_full = lax.all_gather(out_weight, "dp", axis=0, tiled=True)
    mixer_in = (key_loc.astype(F32) * value_loc.astype(F32)).astype(BF16)
    previous = shifted(mixer_in, "ctx", 1)

    tap_index = jnp.arange(taps, dtype=F32)
    decay_env = jnp.exp(-filter_decay[:, None] * tap_index[None, :])
    filter_loc = (filter_taps * decay_env).astype(BF16).astype(F32)
    filt = gather_filters(filter_loc, n_dp, n_ctx)
    width = chans // filt.shape[0]
    block = 2 * LANES

    conv_out, gated = conv_forward(
        offset_loc[:, None], mirror(filt), previous, mixer_in, query_loc, width, block
    )
    rights, lefts = [gated], [gated]
    for step in range(1, n_ctx):
        rights.append(hop(rights[-1], 1, lambda i: i >= step - 1))
        lefts.append(hop(lefts[-1], -1, lambda i: i <= n_ctx - step))
        if step == n_ctx - 2:
            weight_full, rights[step], lefts[step] = lax.optimization_barrier(
                (weight_full, rights[step], lefts[step])
            )

    grad_part = lax.dot_general(
        cotangent, weight_full, (((1,), (1,)), ((), ())), preferred_element_type=F32
    ).astype(BF16)

    gated_full = lax.dynamic_update_slice(
        jnp.zeros((n_ctx * rows, chans), BF16), gated, (me_ctx * rows, 0)
    )
    for step in range(1, n_ctx):
        source = lax.rem(me_ctx - step + n_ctx, n_ctx)
        came = jnp.where(me_ctx >= step, rights[step], lefts[n_ctx - step])
        gated_full = lax.dynamic_update_slice(gated_full, came, (source * rows, 0))
    gated_full, grad_part = lax.optimization_barrier((gated_full, grad_part))

    def block_of(index):
        return lax.dynamic_slice(grad_part, (index * rows, 0), (rows, chans))

    to_right = to_left = None
    for step in range(1, n_ctx):
        send_right = block_of(jnp.minimum(me_ctx + n_ctx - step, n_ctx - 1))
        send_left = block_of(jnp.maximum(me_ctx - n_ctx + step, 0))
        if step > 1:
            send_right = (send_right.astype(F32) + to_right.astype(F32)).astype(BF16)
            send_left = (send_left.astype(F32) + to_left.astype(F32)).astype(BF16)
        to_right = hop(send_right, 1, lambda i: i <= step - 1)
        to_left = hop(send_left, -1, lambda i: i >= n_ctx - step)
    parts = [block_of(me_ctx), to_right, to_left]

    weight_part = lax.dot_general(
        gated_full, cotangent, (((0,), (0,)), ((), ())), preferred_element_type=F32
    ).astype(BF16)
    gated_full, weight_part = lax.optimization_barrier((gated_full, weight_part))
    weight_sum = lax.psum_scatter(weight_part, "dp", scatter_dimension=0, tiled=True)
    mixed = jnp.dot(gated_full, weight_full, preferred_element_type=F32).astype(BF16)
    mixed, parts = lax.optimization_barrier((mixed, parts))

    grad_query, grad_own, spill, lag_sums = conv_backward(
        offset_loc[None, :],
        offset_loc[::-1][:, None],
        filt,
        previous,
        mixer_in,
        query_loc,
        conv_out,
        parts,
        width,
        block,
    )
    grad_mixer = grad_own + shifted(spill, "ctx", -1).astype(F32)
    grad_key = (grad_mixer * value_loc.astype(F32)).astype(BF16)
    grad_value = (grad_mixer * key_loc.astype(F32)).astype(BF16)

    grad_filter = mirror(reduce_filters(lag_sums, n_dp, n_ctx))
    grad_taps = grad_filter * decay_env
    grad_decay = -jnp.sum(tap_index[None, :] * grad_filter * filter_taps * decay_env, axis=1)
    weight_sum, grad_key, grad_value, grad_decay = lax.optimization_barrier(
        (weight_sum, grad_key, grad_value, grad_decay)
    )
    grad_weight = weight_sum.astype(F32)
    return (
        mixed[None],
        grad_query[None],
        grad_key[None],
        grad_value[None],
        grad_weight,
        grad_taps,
        grad_decay,
    )


def solution(mesh):
    in_specs = (
        P("dp", "ctx", None),
        P("dp", "ctx", None),
        P("dp", "ctx", None),
        P("dp", "ctx"),
        P(("dp", "ctx"), None),
        P(("dp", "ctx")),
        P("dp", "ctx"),
        P("dp", None, "ctx"),
    )
    out_specs = (
        P("dp", None, "ctx"),
        P("dp", "ctx", None),
        P("dp", "ctx", None),
        P("dp", "ctx", None),
        P("dp", "ctx"),
        P(("dp", "ctx"), None),
        P(("dp", "ctx")),
    )
    return jax.shard_map(local, mesh=mesh, in_specs=in_specs, out_specs=out_specs, check_vma=False)
```

```python
import functools

import jax
import jax.numpy as jnp
from jax import lax
from jax.experimental import pallas as pl
from jax.experimental.pallas import tpu as pltpu
from jax.sharding import PartitionSpec as P

MESH = pl.DeviceIdType.MESH
F32 = jnp.float32
BF16 = jnp.bfloat16
LANES = 128


def greet(n_dp, n_ctx, me_dp, me_ctx):
    barrier = pltpu.get_barrier_semaphore()
    for step in range(1, n_ctx):
        peer = (me_dp, lax.rem(me_ctx + step, n_ctx))
        pl.semaphore_signal(barrier, inc=1, device_id=peer, device_id_type=MESH)
    for step in range(1, n_dp):
        peer = (lax.rem(me_dp + step, n_dp), me_ctx)
        pl.semaphore_signal(barrier, inc=1, device_id=peer, device_id_type=MESH)
    pl.semaphore_wait(barrier, n_ctx + n_dp - 2)


def gather_kernel(n_dp, n_ctx, x_ref, out_ref, held, send1, recv1, send2, recv2):
    me_dp, me_ctx = lax.axis_index("dp"), lax.axis_index("ctx")
    greet(n_dp, n_ctx, me_dp, me_ctx)
    held[me_dp, me_ctx] = x_ref[...]
    copies = []
    for step in range(1, n_ctx):
        copy = pltpu.make_async_remote_copy(
            src_ref=x_ref,
            dst_ref=held.at[me_dp, me_ctx],
            send_sem=send1.at[step - 1],
            recv_sem=recv1.at[step - 1],
            device_id=(me_dp, lax.rem(me_ctx + step, n_ctx)),
            device_id_type=MESH,
        )
        copy.start()
        copies.append(copy)
    for copy in copies:
        copy.wait()
    copies = []
    for step in range(1, n_dp):
        copy = pltpu.make_async_remote_copy(
            src_ref=held.at[me_dp],
            dst_ref=held.at[me_dp],
            send_sem=send2.at[step - 1],
            recv_sem=recv2.at[step - 1],
            device_id=(lax.rem(me_dp + step, n_dp), me_ctx),
            device_id_type=MESH,
        )
        copy.start()
        copies.append(copy)
    for copy in copies:
        copy.wait()
    out_ref[...] = held[...]


def gather_filters(filter_loc, n_dp, n_ctx):
    rows, taps = filter_loc.shape
    out = pl.pallas_call(
        functools.partial(gather_kernel, n_dp, n_ctx),
        out_shape=jax.ShapeDtypeStruct((n_dp, n_ctx, rows, taps), F32),
        in_specs=[pl.BlockSpec(memory_space=pltpu.VMEM)],
        out_specs=pl.BlockSpec(memory_space=pltpu.VMEM),
        scratch_shapes=[
            pltpu.VMEM((n_dp, n_ctx, rows, taps), F32),
            pltpu.SemaphoreType.DMA((n_ctx - 1,)),
            pltpu.SemaphoreType.DMA((n_ctx - 1,)),
            pltpu.SemaphoreType.DMA((n_dp - 1,)),
            pltpu.SemaphoreType.DMA((n_dp - 1,)),
        ],
        compiler_params=pltpu.CompilerParams(collective_id=0, has_side_effects=True),
    )(filter_loc)
    return out.reshape(n_dp * n_ctx * rows, taps)


def reduce_kernel(n_dp, n_ctx, x_ref, out_ref, got1, part, got2, send1, recv1, send2, recv2):
    me_dp, me_ctx = lax.axis_index("dp"), lax.axis_index("ctx")
    greet(n_dp, n_ctx, me_dp, me_ctx)
    copies = []
    for step in range(1, n_ctx):
        peer = lax.rem(me_ctx + step, n_ctx)
        copy = pltpu.make_async_remote_copy(
            src_ref=x_ref.at[peer],
            dst_ref=got1.at[step - 1],
            send_sem=send1.at[step - 1],
            recv_sem=recv1.at[step - 1],
            device_id=(me_dp, peer),
            device_id_type=MESH,
        )
        copy.start()
        copies.append(copy)
    for copy in copies:
        copy.wait()
    total = x_ref[me_ctx]
    for step in range(1, n_ctx):
        total = total + got1[step - 1]
    part[...] = total
    copies = []
    for step in range(1, n_dp):
        peer = lax.rem(me_dp + step, n_dp)
        copy = pltpu.make_async_remote_copy(
            src_ref=part.at[peer],
            dst_ref=got2.at[step - 1],
            send_sem=send2.at[step - 1],
            recv_sem=recv2.at[step - 1],
            device_id=(peer, me_ctx),
            device_id_type=MESH,
        )
        copy.start()
        copies.append(copy)
    for copy in copies:
        copy.wait()
    total = part[me_dp]
    for step in range(1, n_dp):
        total = total + got2[step - 1]
    out_ref[...] = total


def reduce_filters(grad_filter, n_dp, n_ctx):
    groups, taps = grad_filter.shape
    rows = groups // (n_dp * n_ctx)
    blocks = grad_filter.reshape(n_dp, n_ctx, rows, taps).transpose(1, 0, 2, 3)
    return pl.pallas_call(
        functools.partial(reduce_kernel, n_dp, n_ctx),
        out_shape=jax.ShapeDtypeStruct((rows, taps), F32),
        in_specs=[pl.BlockSpec(memory_space=pltpu.VMEM)],
        out_specs=pl.BlockSpec(memory_space=pltpu.VMEM),
        scratch_shapes=[
            pltpu.VMEM((n_ctx - 1, n_dp, rows, taps), F32),
            pltpu.VMEM((n_dp, rows, taps), F32),
            pltpu.VMEM((n_dp - 1, rows, taps), F32),
            pltpu.SemaphoreType.DMA((n_ctx - 1,)),
            pltpu.SemaphoreType.DMA((n_ctx - 1,)),
            pltpu.SemaphoreType.DMA((n_dp - 1,)),
            pltpu.SemaphoreType.DMA((n_dp - 1,)),
        ],
        compiler_params=pltpu.CompilerParams(collective_id=1, has_side_effects=True),
    )(blocks)


def circulant(row):
    size = row.shape[1]
    return pltpu.roll(
        jnp.broadcast_to(row, (size, size)), 0, 1, stride=1, stride_axis=0
    )


def grids(size):
    return (
        lax.broadcasted_iota(jnp.int32, (size, size), 0),
        lax.broadcasted_iota(jnp.int32, (size, size), 1),
    )


def forward_kernel(width, off_ref, filt_ref, prev_ref, mix_ref, query_ref, conv_ref, gated_ref):
    size = LANES
    t_index, u_index = grids(size)
    off = jnp.broadcast_to(off_ref[...], (size, size))
    own = (u_index <= t_index) & (t_index - u_index <= off)
    before = (u_index > t_index) & (t_index + size - u_index <= off)
    per_tile = LANES // width
    lane_group = lax.broadcasted_iota(jnp.int32, (2 * size, LANES), 1) // width
    for tile in range(mix_ref.shape[1] // LANES):
        cols = slice(tile * LANES, (tile + 1) * LANES)
        mixer = jnp.concatenate([prev_ref[:, cols], mix_ref[:, cols]], axis=0)
        total = jnp.zeros((size, LANES), F32)
        for index in range(per_tile):
            group = tile * per_tile + index
            ring = circulant(filt_ref[group : group + 1, :])
            band = jnp.concatenate(
                [jnp.where(before, ring, 0.0).astype(BF16), jnp.where(own, ring, 0.0).astype(BF16)],
                axis=1,
            )
            picked = jnp.where(lane_group == index, mixer, jnp.zeros((), BF16))
            total = total + jnp.dot(band, picked, preferred_element_type=F32)
        conv_ref[:, cols] = total
        gated_ref[:, cols] = (query_ref[:, cols].astype(F32) * total).astype(BF16)


def conv_forward(offset_col, filt_rev, previous, mixer_in, query, width, block):
    rows, chans = mixer_in.shape
    groups = block // width
    spec = pl.BlockSpec((rows, block), lambda i: (0, i))
    return pl.pallas_call(
        functools.partial(forward_kernel, width),
        grid=(chans // block,),
        out_shape=(
            jax.ShapeDtypeStruct((rows, chans), F32),
            jax.ShapeDtypeStruct((rows, chans), BF16),
        ),
        in_specs=[
            pl.BlockSpec((rows, 1), lambda i: (0, 0)),
            pl.BlockSpec((groups, rows), lambda i: (i, 0)),
            spec,
            spec,
            spec,
        ],
        out_specs=(spec, spec),
        cost_estimate=pl.CostEstimate(
            flops=4 * rows * rows * LANES * (chans // width),
            bytes_accessed=12 * rows * chans,
            transcendentals=0,
        ),
    )(offset_col, filt_rev, previous, mixer_in, query)


def backward_kernel(
    width, parts, off_row_ref, off_flip_ref, filt_ref, prev_ref, mix_ref, query_ref, conv_ref, *rest
):
    part_refs = rest[:parts]
    gquery_ref, gmix_ref, spill_ref, gfilt_ref = rest[parts:]
    size = LANES
    u_index, t_index = grids(size)
    off = jnp.broadcast_to(off_row_ref[...], (size, size))
    own = (u_index <= t_index) & (t_index - u_index <= off)
    before = (u_index > t_index) & (t_index + size - u_index <= off)
    flip_row, lag_col = grids(size)
    flip_t = size - 1 - flip_row
    off_flip = jnp.broadcast_to(off_flip_ref[...], (size, size))
    own_flip = (lag_col <= flip_t) & (flip_t - lag_col <= off_flip)
    before_flip = (lag_col > flip_t) & (flip_t + size - lag_col <= off_flip)
    flip = jnp.where(flip_row + lag_col == size - 1, 1.0, 0.0).astype(BF16)
    per_tile = LANES // width
    lane_group = lax.broadcasted_iota(jnp.int32, (size, LANES), 1) // width
    zero = jnp.zeros((), BF16)
    for tile in range(mix_ref.shape[1] // LANES):
        cols = slice(tile * LANES, (tile + 1) * LANES)
        mixer = jnp.concatenate([prev_ref[:, cols], mix_ref[:, cols]], axis=0)
        gated_grad = part_refs[0][:, cols].astype(F32)
        for ref in part_refs[1:]:
            gated_grad = gated_grad + ref[:, cols].astype(F32)
        gquery_ref[:, cols] = (gated_grad * conv_ref[:, cols]).astype(BF16)
        gconv = (gated_grad * query_ref[:, cols].astype(F32)).astype(BF16)
        flipped = jnp.dot(flip, gconv, preferred_element_type=F32).astype(BF16)
        total = jnp.zeros((2 * size, LANES), F32)
        for pair in range(per_tile // 2):
            bands, picks = [], []
            for index in (2 * pair, 2 * pair + 1):
                group = tile * per_tile + index
                ring = circulant(filt_ref[group : group + 1, :])
                bands.append(
                    jnp.concatenate(
                        [
                            jnp.where(before, ring, 0.0).astype(BF16),
                            jnp.where(own, ring, 0.0).astype(BF16),
                        ],
                        axis=0,
                    )
                )
                picks.append(jnp.where(lane_group == index, gconv, zero))
                product = lax.dot_general(
                    jnp.where(lane_group == index, flipped, zero),
                    mixer,
                    (((1,), (1,)), ((), ())),
                    preferred_element_type=F32,
                )
                folded = jnp.where(
                    own_flip,
                    product[:, size:],
                    jnp.where(before_flip, product[:, :size], 0.0),
                )
                aligned = pltpu.roll(folded, 1, 1, stride=1, stride_axis=0)
                gfilt_ref[group : group + 1, :] = jnp.sum(aligned, axis=0, keepdims=True)
            total = total + jnp.dot(
                jnp.concatenate(bands, axis=1),
                jnp.concatenate(picks, axis=0),
                preferred_element_type=F32,
            )
        spill_ref[:, cols] = total[:size].astype(BF16)
        gmix_ref[:, cols] = total[size:]


def conv_backward(
    offset_row, offset_flip, filt, previous, mixer_in, query, conv_out, parts, width, block
):
    rows, chans = mixer_in.shape
    groups = block // width
    spec = pl.BlockSpec((rows, block), lambda i: (0, i))
    filt_spec = pl.BlockSpec((groups, rows), lambda i: (i, 0))
    return pl.pallas_call(
        functools.partial(backward_kernel, width, len(parts)),
        grid=(chans // block,),
        out_shape=(
            jax.ShapeDtypeStruct((rows, chans), BF16),
            jax.ShapeDtypeStruct((rows, chans), F32),
            jax.ShapeDtypeStruct((rows, chans), BF16),
            jax.ShapeDtypeStruct((chans // width, rows), F32),
        ),
        in_specs=[
            pl.BlockSpec((1, rows), lambda i: (0, 0)),
            pl.BlockSpec((rows, 1), lambda i: (0, 0)),
            filt_spec,
            spec,
            spec,
            spec,
            spec,
        ]
        + [spec] * len(parts),
        out_specs=(spec, spec, spec, filt_spec),
        cost_estimate=pl.CostEstimate(
            flops=8 * rows * rows * LANES * (chans // width),
            bytes_accessed=28 * rows * chans,
            transcendentals=0,
        ),
    )(offset_row, offset_flip, filt, previous, mixer_in, query, conv_out, *parts)


def shifted(value, axis, by):
    length = lax.axis_size(axis)
    pairs = [(i, i + by) for i in range(length) if 0 <= i + by < length]
    return lax.ppermute(value, axis, pairs)


def hop(value, by, sends):
    length = lax.axis_size("ctx")
    pairs = [(i, i + by) for i in range(length) if 0 <= i + by < length and sends(i)]
    return lax.ppermute(value, "ctx", pairs)


def mirror(rows):
    return jnp.concatenate([rows[:, :1], rows[:, :0:-1]], axis=1)


def local(
    query_proj, key_proj, value_proj, offsets, filter_taps, filter_decay, out_weight, grad_mixed
):
    n_dp, n_ctx = lax.axis_size("dp"), lax.axis_size("ctx")
    me_ctx = lax.axis_index("ctx")
    query_loc = query_proj[0]
    key_loc = key_proj[0]
    value_loc = value_proj[0]
    offset_loc = offsets[0]
    cotangent = grad_mixed[0]
    rows, chans = query_loc.shape
    taps = filter_taps.shape[1]

    weight_full = lax.all_gather(out_weight, "dp", axis=0, tiled=True)
    mixer_in = (key_loc.astype(F32) * value_loc.astype(F32)).astype(BF16)
    previous = shifted(mixer_in, "ctx", 1)

    tap_index = jnp.arange(taps, dtype=F32)
    decay_env = jnp.exp(-filter_decay[:, None] * tap_index[None, :])
    filter_loc = (filter_taps * decay_env).astype(BF16).astype(F32)
    filt = gather_filters(filter_loc, n_dp, n_ctx)
    width = chans // filt.shape[0]
    block = 2 * LANES

    conv_out, gated = conv_forward(
        offset_loc[:, None], mirror(filt), previous, mixer_in, query_loc, width, block
    )
    rights, lefts = [gated], [gated]
    for step in range(1, n_ctx):
        rights.append(hop(rights[-1], 1, lambda i: i >= step - 1))
        lefts.append(hop(lefts[-1], -1, lambda i: i <= n_ctx - step))
        if step == n_ctx - 2:
            weight_full, rights[step], lefts[step] = lax.optimization_barrier(
                (weight_full, rights[step], lefts[step])
            )

    grad_part = lax.dot_general(
        cotangent, weight_full, (((1,), (1,)), ((), ())), preferred_element_type=F32
    ).astype(BF16)

    first_right = lax.dynamic_slice(grad_part, ((n_ctx - 1) * rows, 0), (rows, chans))
    first_left = lax.dynamic_slice(grad_part, (0, 0), (rows, chans))
    to_right = hop(first_right, 1, lambda i: i <= 0)
    to_left = hop(first_left, -1, lambda i: i >= n_ctx - 1)
    gated_full = lax.dynamic_update_slice(
        jnp.zeros((n_ctx * rows, chans), BF16), gated, (me_ctx * rows, 0)
    )
    for step in range(1, n_ctx):
        source = lax.rem(me_ctx - step + n_ctx, n_ctx)
        came = jnp.where(me_ctx >= step, rights[step], lefts[n_ctx - step])
        gated_full = lax.dynamic_update_slice(gated_full, came, (source * rows, 0))
    gated_full, grad_part, to_right, to_left = lax.optimization_barrier(
        (gated_full, grad_part, to_right, to_left)
    )

    def block_of(index):
        return lax.dynamic_slice(grad_part, (index * rows, 0), (rows, chans))

    for step in range(2, n_ctx):
        send_right = block_of(jnp.minimum(me_ctx + n_ctx - step, n_ctx - 1))
        send_left = block_of(jnp.maximum(me_ctx - n_ctx + step, 0))
        send_right = (send_right.astype(F32) + to_right.astype(F32)).astype(BF16)
        send_left = (send_left.astype(F32) + to_left.astype(F32)).astype(BF16)
        to_right = hop(send_right, 1, lambda i: i <= step - 1)
        to_left = hop(send_left, -1, lambda i: i >= n_ctx - step)
    parts = [block_of(me_ctx), to_right, to_left]

    weight_part = lax.dot_general(
        gated_full, cotangent, (((0,), (0,)), ((), ())), preferred_element_type=F32
    ).astype(BF16)
    gated_full, weight_part = lax.optimization_barrier((gated_full, weight_part))
    weight_sum = lax.psum_scatter(weight_part, "dp", scatter_dimension=0, tiled=True)
    mixed = jnp.dot(gated_full, weight_full, preferred_element_type=F32).astype(BF16)
    mixed, parts = lax.optimization_barrier((mixed, parts))

    grad_query, grad_own, spill, lag_sums = conv_backward(
        offset_loc[None, :],
        offset_loc[::-1][:, None],
        filt,
        previous,
        mixer_in,
        query_loc,
        conv_out,
        parts,
        width,
        block,
    )
    grad_mixer = grad_own + shifted(spill, "ctx", -1).astype(F32)
    grad_key = (grad_mixer * value_loc.astype(F32)).astype(BF16)
    grad_value = (grad_mixer * key_loc.astype(F32)).astype(BF16)

    grad_filter = mirror(reduce_filters(lag_sums, n_dp, n_ctx))
    grad_taps = grad_filter * decay_env
    grad_decay = -jnp.sum(tap_index[None, :] * grad_filter * filter_taps * decay_env, axis=1)
    weight_sum, grad_key, grad_value, grad_decay = lax.optimization_barrier(
        (weight_sum, grad_key, grad_value, grad_decay)
    )
    grad_weight = weight_sum.astype(F32)
    return (
        mixed[None],
        grad_query[None],
        grad_key[None],
        grad_value[None],
        grad_weight,
        grad_taps,
        grad_decay,
    )


def solution(mesh):
    in_specs = (
        P("dp", "ctx", None),
        P("dp", "ctx", None),
        P("dp", "ctx", None),
        P("dp", "ctx"),
        P(("dp", "ctx"), None),
        P(("dp", "ctx")),
        P("dp", "ctx"),
        P("dp", None, "ctx"),
    )
    out_specs = (
        P("dp", None, "ctx"),
        P("dp", "ctx", None),
        P("dp", "ctx", None),
        P("dp", "ctx", None),
        P("dp", "ctx"),
        P(("dp", "ctx"), None),
        P(("dp", "ctx")),
    )
    return jax.shard_map(local, mesh=mesh, in_specs=in_specs, out_specs=out_specs, check_vma=False)
```
